1024 devices in a mesh: row: 64 (over z_hi, y, core), col: 16 (over x, z_lo).
Axes of the slice: x: 8, y: 8, z: 8 (z_hi: 4, z_lo: 2; z = z_hi * 2 + z_lo), core: 2. Of those that a mesh axis runs over, the one named last changes fastest.
Arguments:
- a_tiles: float32 [64, 16, 3, 256, 256], P('row', 'col'), may hold values from -0.375 to 0.375
- b_tiles: float32 [64, 16, 3, 256, 256], P('row', 'col'), may hold values from -6 to 6
- a_rows: int32 [64, 16, 3], P('row', 'col'), may hold values from 0 to 7, as said below
- b_cols: int32 [64, 16, 3], P('row', 'col'), may hold values from 0 to 31, as said below
- c_shape: int32 [64, 16, 6, 2], P('row', 'col'), may hold values from 0 to 31, as said below
- pairs: int32 [64, 16, 3, 6, 2], P('row', 'col'), may hold values from 0 to 2, as said below
- pair_count: int32 [64, 16, 3], P('row', 'col'), may hold values from 1 to 6, as said below
Outputs:
- c_tiles: float32 [64, 16, 6, 256, 256], P('row', 'col')
The draws below stay inside these ranges and needn't reach their ends.
Inputs may be any that keep to these rules, and one draw needn't show every extreme that they name: `a_rows`: in each row block every device's A slots name the same 3 distinct tile rows, each device in its own order. `b_cols`: in each column block every device's B slots name the same 3 distinct tile columns, each device in its own order. `c_shape`: each device's result slots are distinct combinations of its row block's A tile rows and its column block's B tile columns. The first pair_count pairs of a device and step are live; live pairs of one step have distinct targets, and every target appears in c_shape. `pair_count`: some device and step lists all 6 pairs.
All inputs are finite; a program needn't handle non-finite values.
Results may differ from the reference program's by a relative error of at most 0.0003.
Values sent between devices are 32-bit elements; how exact they have to be, the bound alone decides.
No kernel may reach another device: no remote copies, remote signals or barrier semaphores. Data moves between devices by JAX's collectives and lax.ppermute only.
A program may use at most 32 MiB of HBM per device.

```python
import jax
import jax.numpy as jnp
from jax import lax

TILE = 256
ROW_TILES = 8
COL_TILES = 32
SLOTS = 3
CSLOTS = 6
STEPS = 3
N_ROW = 64
N_COL = 16


def permuted(key, count, total, take):
    subkeys = jax.random.split(key, count)
    return jax.vmap(lambda subkey: jax.random.permutation(subkey, total)[:take])(subkeys).astype(jnp.int32)


def with_largest(sets, largest):
    present = jnp.any(sets[0] == largest)
    first_value = jnp.where(present, sets[0, 0], largest).astype(jnp.int32)
    return sets.at[0, 0].set(first_value)


def layout(key):
    folded = jax.random.fold_in(key, 11)
    subkeys = jax.random.split(folded, 8)
    device_count = N_ROW * N_COL
    set_rows = with_largest(permuted(subkeys[0], N_ROW, ROW_TILES, SLOTS), ROW_TILES - 1)
    set_cols = with_largest(permuted(subkeys[1], N_COL, COL_TILES, SLOTS), COL_TILES - 1)
    order_a = permuted(subkeys[2], device_count, SLOTS, SLOTS).reshape(N_ROW, N_COL, SLOTS)
    order_b = permuted(subkeys[3], device_count, SLOTS, SLOTS).reshape(N_ROW, N_COL, SLOTS)
    rows_wide = jnp.broadcast_to(set_rows[:, None, :], (N_ROW, N_COL, SLOTS))
    cols_wide = jnp.broadcast_to(set_cols[None, :, :], (N_ROW, N_COL, SLOTS))
    a_rows = jnp.take_along_axis(rows_wide, order_a, axis=2)
    b_cols = jnp.take_along_axis(cols_wide, order_b, axis=2)
    combos = permuted(subkeys[4], device_count, SLOTS * SLOTS, CSLOTS).reshape(N_ROW, N_COL, CSLOTS)
    canon_a = combos // SLOTS
    canon_b = combos % SLOTS
    c_row = jnp.take_along_axis(rows_wide, canon_a, axis=2)
    c_col = jnp.take_along_axis(cols_wide, canon_b, axis=2)
    c_shape = jnp.stack([c_row, c_col], axis=-1).astype(jnp.int32)
    inverse_a = jnp.argsort(order_a[:, :STEPS, :], axis=-1, stable=True).astype(jnp.int32)
    inverse_b = jnp.argsort(order_b[:STEPS, :, :], axis=-1, stable=True).astype(jnp.int32)
    inverse_a_wide = jnp.broadcast_to(inverse_a[:, None, :, :], (N_ROW, N_COL, STEPS, SLOTS))
    inverse_b_wide = jnp.broadcast_to(jnp.transpose(inverse_b, (1, 0, 2))[None], (N_ROW, N_COL, STEPS, SLOTS))
    chosen = permuted(subkeys[5], device_count * STEPS, CSLOTS, CSLOTS).reshape(N_ROW, N_COL, STEPS, CSLOTS)
    canon_a_wide = jnp.broadcast_to(canon_a[:, :, None, :], (N_ROW, N_COL, STEPS, CSLOTS))
    canon_b_wide = jnp.broadcast_to(canon_b[:, :, None, :], (N_ROW, N_COL, STEPS, CSLOTS))
    pick_a = jnp.take_along_axis(canon_a_wide, chosen, axis=3)
    pick_b = jnp.take_along_axis(canon_b_wide, chosen, axis=3)
    a_slot = jnp.take_along_axis(inverse_a_wide, pick_a, axis=3)
    b_slot = jnp.take_along_axis(inverse_b_wide, pick_b, axis=3)
    pairs = jnp.stack([a_slot, b_slot], axis=-1).astype(jnp.int32)
    counts = jax.random.randint(subkeys[6], (device_count * STEPS,), 1, CSLOTS + 1)
    forced = jax.random.randint(subkeys[7], (), 0, device_count * STEPS)
    counts = jnp.where(jnp.arange(device_count * STEPS) == forced, CSLOTS, counts)
    counts = counts.reshape(N_ROW, N_COL, STEPS).astype(jnp.int32)
    return (a_rows.astype(jnp.int32), b_cols.astype(jnp.int32), c_shape, pairs, counts)


def draw_a_rows(key, part):
    return layout(key)[0]


def draw_b_cols(key, part):
    return layout(key)[1]


def draw_c_shape(key, part):
    return layout(key)[2]


def draw_pairs(key, part):
    return layout(key)[3]


def draw_pair_count(key, part):
    return layout(key)[4]


def block_levels(key, shape, pieces, smallest, high):
    factor_of, own = 1.0, jax.random.fold_in(key, 6)
    for axis_at, parts in pieces:
        steps = jnp.exp(jax.random.uniform(jax.random.fold_in(own, axis_at), (parts,), jnp.float32, smallest / len(pieces), high / len(pieces)))
        factor_of = factor_of * jnp.repeat(steps, shape[axis_at] // parts).reshape([-1 if axis == axis_at else 1 for axis in range(len(shape))])
    return factor_of


def gaussian(rng, extent, deviation, reach, cuts=(), dtype=jnp.bfloat16):
    values = deviation * jax.random.normal(rng, extent, jnp.float32)
    if cuts:
        values = values * block_levels(rng, extent, cuts, -0.22, 0.18)
    return jnp.clip(values, -reach, reach).astype(dtype)


def setup_inputs(seed: int = 0) -> dict:
    arg_keys = jax.random.split(jax.random.key(seed), 8)
    return {
        "a_tiles": gaussian(arg_keys[0], (N_ROW, N_COL, SLOTS, TILE, TILE), TILE ** -0.5, 0.375, ((0, 64), (1, 16)), jnp.float32),
        "b_tiles": gaussian(arg_keys[1], (N_ROW, N_COL, SLOTS, TILE, TILE), 1.0, 6.0, ((0, 64), (1, 16)), jnp.float32),
        "a_rows": draw_a_rows(jax.random.fold_in(arg_keys[7], 71), 0),
        "b_cols": draw_b_cols(jax.random.fold_in(arg_keys[7], 71), 0),
        "c_shape": draw_c_shape(jax.random.fold_in(arg_keys[7], 71), 0),
        "pairs": draw_pairs(jax.random.fold_in(arg_keys[7], 71), 0),
        "pair_count": draw_pair_count(jax.random.fold_in(arg_keys[7], 71), 0),
    }


def reference(a_tiles, b_tiles, a_rows, b_cols, c_shape, pairs, pair_count):
    def device_block(index):
        row_index = index // N_COL
        col_index = index % N_COL
        c_row = c_shape[row_index, col_index, :, 0]
        c_col = c_shape[row_index, col_index, :, 1]
        result = jnp.zeros((CSLOTS, TILE, TILE), jnp.float32)
        for step in range(STEPS):
            a_panel = a_tiles[row_index, step]
            row_list = a_rows[row_index, step]
            b_panel = b_tiles[step, col_index]
            col_list = b_cols[step, col_index]
            a_pick = pairs[row_index, col_index, step, :, 0]
            b_pick = pairs[row_index, col_index, step, :, 1]
            active = jnp.arange(CSLOTS) < pair_count[row_index, col_index, step]
            target = (row_list[a_pick][:, None] == c_row[None, :]) & (col_list[b_pick][:, None] == c_col[None, :]) & active[:, None]
            products = jnp.einsum("pik,pkj->pij", a_panel[a_pick], b_panel[b_pick], precision=lax.Precision.HIGHEST)
            result = result + jnp.einsum("pl,pij->lij", target.astype(jnp.float32), products, precision=lax.Precision.HIGHEST)
        return result

    blocks = lax.map(device_block, jnp.arange(N_ROW * N_COL))
    return blocks.reshape(N_ROW, N_COL, CSLOTS, TILE, TILE)
```

```python
import jax
import jax.numpy as jnp
from jax import lax
from jax.experimental import pallas as pl
from jax.experimental.pallas import tpu as pltpu
from jax.sharding import PartitionSpec as P


STEPS, SLOTS, SIDE, RESULTS = 3, 3, 256, 6
RING, PAIR, PLANES = 8, 2, 4
SHARD = 160
SHARDS = 5
PANEL = SHARD * SHARDS
LIST_ROW = SLOTS * SIDE

HOLDERS = (
    ((0, 0), (0, 1), (7, 0), (6, 0), (5, 0)),
    ((6, 1), (7, 1), (2, 1), (3, 1), (4, 1)),
    ((1, 0), (1, 1), (2, 0), (3, 0), (4, 0)),
)
HOLDER = tuple(tuple(ring * PAIR + pair for ring, pair in panel) for panel in HOLDERS)
SLOT_OF = [STEPS * SHARDS] * (RING * PAIR)
for _s in range(STEPS):
    for _k in range(SHARDS):
        SLOT_OF[HOLDER[_s][_k]] = _s * SHARDS + _k

SCATTER = [
    [(s, HOLDER[s][k]) for s in range(STEPS) if HOLDER[s][k] != s] for k in range(SHARDS)
]


def ring_x(step):
    return [(x * PAIR + z, (x + step) % RING * PAIR + z) for x in range(RING) for z in range(PAIR)]


def ring_y(step):
    pairs = []
    for z in range(PLANES):
        for y in range(RING):
            for core in range(PAIR):
                to = (y + (step if core == 0 else -step)) % RING
                pairs.append(((z * RING + y) * PAIR + core, (z * RING + to) * PAIR + core))
    return pairs


SWAP_Z = [(c, c ^ 1) for c in range(RING * PAIR)]
SWAP_CORE = [(r, r ^ 1) for r in range(PLANES * RING * PAIR)]


def to_plane(z):
    return [(r, z * RING * PAIR + r) for r in range(RING * PAIR)]


def scatter(tiles, listed, axis, index):
    panel = tiles.reshape(SLOTS * SIDE, SIDE)
    spare = jnp.pad(listed.astype(jnp.float32)[None, :], ((0, PANEL - LIST_ROW - 1), (0, SIDE - SLOTS)))
    shards = [panel[k * SHARD : (k + 1) * SHARD] for k in range(SHARDS - 1)]
    shards.append(jnp.concatenate([panel[(SHARDS - 1) * SHARD :], spare]))
    arrived = [lax.ppermute(shards[k], axis, SCATTER[k]) for k in range(SHARDS)]
    keeps = jnp.logical_or(index == HOLDER[0][0], index == HOLDER[2][0])
    return jnp.where(keeps, shards[0], sum(arrived[1:], arrived[0]))


def kernel(ints, *refs):
    a_refs, b_refs = refs[:9], refs[9:15]
    out, a_all, b_all, a_sp, b_sp, lists, sems, list_sems = refs[15:]
    col, row = ints[51], ints[52]
    x, z = lax.div(col, 2), lax.rem(col, 2)
    y, core = lax.rem(lax.div(row, 2), RING), lax.rem(row, 2)

    copies = []

    def place(ref, part, dest, origin):
        slot = ints[53 + origin]
        copy = pltpu.make_async_copy(
            ref.at[pl.ds(part * SHARD, SHARD), :],
            dest.at[pl.ds(pl.multiple_of(slot * SHARD, SHARD), SHARD), :],
            sems.at[len(copies)],
        )
        copy.start()
        copies.append(copy)

    for half in range(2):
        core_of = core if half == 0 else 1 - core
        way = 1 - 2 * core_of
        for ref, first, count in zip(b_refs[3 * half : 3 * half + 3], (-4, -1, 2), (3, 3, 2)):
            for part in range(count):
                origin_y = lax.rem(y + way * (first + part) + 2 * RING, RING)
                place(ref, part, b_all, origin_y * PAIR + core_of)
    for ref, shift in zip(a_refs[:7], (0, -1, 1, -2, 2, -3, 3)):
        origin_x = lax.rem(x + shift + RING, RING)
        place(ref, 0, a_all, origin_x * PAIR + z)
        place(ref, 1, a_all, origin_x * PAIR + (1 - z))
    far = lax.rem(x + 4, RING)
    place(a_refs[7], 0, a_all, far * PAIR + z)
    place(a_refs[8], 0, a_all, far * PAIR + (1 - z))
    for copy in copies:
        copy.wait()

    list_copies = []
    for s in range(STEPS):
        for which, source in enumerate((a_all, b_all)):
            copy = pltpu.make_async_copy(
                source.at[pl.ds(s * PANEL + LIST_ROW, 8), pl.ds(0, 128)],
                lists.at[which * STEPS + s],
                list_sems.at[which * STEPS + s],
            )
            copy.start()
            list_copies.append(copy)

    for source, split in ((a_all, a_sp), (b_all, b_sp)):
        for s in range(STEPS):
            for t in range(SLOTS):
                value = source[pl.ds(s * PANEL + t * SIDE, SIDE), :]
                high = value.astype(jnp.bfloat16)
                split[0, s * SLOTS + t] = high
                split[1, s * SLOTS + t] = (value - high.astype(jnp.float32)).astype(jnp.bfloat16)

    for copy in list_copies:
        copy.wait()

    for l in range(RESULTS):
        c_row, c_col = ints[2 * l], ints[2 * l + 1]
        total = None
        for s in range(STEPS):
            i, j = jnp.int32(0), jnp.int32(0)
            for t in range(SLOTS):
                i = jnp.where(lists[s, 0, t].astype(jnp.int32) == c_row, t, i)
                j = jnp.where(lists[STEPS + s, 0, t].astype(jnp.int32) == c_col, t, j)
            live = jnp.int32(0)
            for p in range(RESULTS):
                at = 12 + (s * RESULTS + p) * 2
                hit = (ints[at] == i) & (ints[at + 1] == j) & (p < ints[48 + s])
                live = jnp.where(hit, 1, live)
            ia, jb = s * SLOTS + i, s * SLOTS + j
            a_high, a_low = a_sp[0, ia], a_sp[1, ia]
            b_high, b_low = b_sp[0, jb], b_sp[1, jb]
            product = (
                jnp.dot(a_high, b_high, preferred_element_type=jnp.float32)
                + jnp.dot(a_high, b_low, preferred_element_type=jnp.float32)
                + jnp.dot(a_low, b_high, preferred_element_type=jnp.float32)
            )
            product = product * live.astype(jnp.float32)
            total = product if total is None else total + product
        out[l] = total


def multiply(ints, a_blocks, b_blocks):
    anywhere = pl.BlockSpec(memory_space=pl.ANY)
    count = len(a_blocks) + len(b_blocks)
    rows = (STEPS * SHARDS + 1) * SHARD
    return pl.pallas_call(
        kernel,
        out_shape=jax.ShapeDtypeStruct((RESULTS, SIDE, SIDE), jnp.float32),
        in_specs=[pl.BlockSpec(memory_space=pltpu.SMEM)] + [anywhere] * count,
        out_specs=pl.BlockSpec(memory_space=pltpu.VMEM),
        scratch_shapes=[
            pltpu.VMEM((rows, SIDE), jnp.float32),
            pltpu.VMEM((rows, SIDE), jnp.float32),
            pltpu.VMEM((2, STEPS * SLOTS, SIDE, SIDE), jnp.bfloat16),
            pltpu.VMEM((2, STEPS * SLOTS, SIDE, SIDE), jnp.bfloat16),
            pltpu.SMEM((2 * STEPS, 8, 128), jnp.float32),
            pltpu.SemaphoreType.DMA((32,)),
            pltpu.SemaphoreType.DMA((2 * STEPS,)),
        ],
        compiler_params=pltpu.CompilerParams(vmem_limit_bytes=24 << 20),
    )(ints, *a_blocks, *b_blocks)


def per_device(a_tiles, b_tiles, a_rows, b_cols, c_shape, pairs, pair_count):
    col, row = lax.axis_index("col"), lax.axis_index("row")
    ints = jnp.concatenate(
        [
            c_shape.reshape(-1),
            pairs.reshape(-1),
            pair_count.reshape(-1),
            col.astype(jnp.int32)[None],
            row.astype(jnp.int32)[None],
            jnp.array(SLOT_OF, jnp.int32),
        ]
    )

    a_own = scatter(a_tiles[0, 0], a_rows[0, 0], "col", col)
    b_first = scatter(b_tiles[0, 0], b_cols[0, 0], "row", row)
    b_own = b_first + sum(lax.ppermute(b_first, "row", to_plane(z)) for z in range(1, PLANES))

    block = jnp.concatenate([a_own, lax.ppermute(a_own, "col", SWAP_Z)])
    lefts, rights = [block], [block]
    for _ in range(3):
        left = lax.ppermute(lefts[-1], "col", ring_x(1))
        right = lax.ppermute(rights[-1], "col", ring_x(-1))
        lefts.append(left)
        rights.append(right)
    far_same = lax.ppermute(lefts[-1][:SHARD], "col", ring_x(1))
    far_other = lax.ppermute(rights[-1][SHARD:], "col", ring_x(-1))
    a_blocks = [block, lefts[1], rights[1], lefts[2], rights[2], lefts[3], rights[3], far_same, far_other]

    behind = lax.ppermute(b_own, "row", ring_y(1))
    ahead = lax.ppermute(b_own, "row", ring_y(-1))
    near = jnp.concatenate([behind, b_own, ahead])
    back = lax.ppermute(near, "row", ring_y(3))
    front = lax.ppermute(near[: 2 * SHARD], "row", ring_y(-3))
    mine = [back, near, front]
    b_blocks = mine + [lax.ppermute(part, "row", SWAP_CORE) for part in mine]

    return multiply(ints, a_blocks, b_blocks)[None, None]


def solution(mesh):
    return jax.shard_map(
        per_device,
        mesh=mesh,
        in_specs=(
            P("row", "col", None, None, None),
            P("row", "col", None, None, None),
            P("row", "col", None),
            P("row", "col", None),
            P("row", "col", None, None),
            P("row", "col", None, None, None),
            P("row", "col", None),
        ),
        out_specs=P("row", "col", None, None, None),
        check_vma=False,
    )
```

```python
import jax
import jax.numpy as jnp
from jax import lax
from jax.experimental import pallas as pl
from jax.experimental.pallas import tpu as pltpu
from jax.sharding import PartitionSpec as P


STEPS, SLOTS, SIDE, RESULTS = 3, 3, 256, 6
RING, PAIR, PLANES = 8, 2, 4
SHARD = 160
SHARDS = 5
PANEL = SHARD * SHARDS
LIST_ROW = SLOTS * SIDE

HOLDERS = (
    ((0, 0), (0, 1), (7, 0), (6, 0), (5, 0)),
    ((6, 1), (7, 1), (2, 1), (3, 1), (4, 1)),
    ((1, 0), (1, 1), (2, 0), (3, 0), (4, 0)),
)
HOLDER = tuple(tuple(ring * PAIR + pair for ring, pair in panel) for panel in HOLDERS)
SLOT_OF = [STEPS * SHARDS] * (RING * PAIR)
for _s in range(STEPS):
    for _k in range(SHARDS):
        SLOT_OF[HOLDER[_s][_k]] = _s * SHARDS + _k

SCATTER = [
    [(s, HOLDER[s][k]) for s in range(STEPS) if HOLDER[s][k] != s] for k in range(SHARDS)
]


def ring_x():
    columns = RING * PAIR
    pairs = []
    for r in range(PLANES * RING * PAIR):
        for c in range(columns):
            to = (c + (PAIR if r % PAIR == 0 else -PAIR)) % columns
            pairs.append((r * columns + c, r * columns + to))
    return pairs


def ring_y(step):
    pairs = []
    for z in range(PLANES):
        for y in range(RING):
            for core in range(PAIR):
                to = (y + (step if core == 0 else -step)) % RING
                pairs.append(((z * RING + y) * PAIR + core, (z * RING + to) * PAIR + core))
    return pairs


SWAP_Z = [(c, c ^ 1) for c in range(RING * PAIR)]
SWAP_CORE = [(r, r ^ 1) for r in range(PLANES * RING * PAIR)]


def to_plane(z):
    return [(r, z * RING * PAIR + r) for r in range(RING * PAIR)]


def scatter(tiles, listed, axis, index):
    panel = tiles.reshape(SLOTS * SIDE, SIDE)
    spare = jnp.pad(listed.astype(jnp.float32)[None, :], ((0, PANEL - LIST_ROW - 1), (0, SIDE - SLOTS)))
    shards = [panel[k * SHARD : (k + 1) * SHARD] for k in range(SHARDS - 1)]
    shards.append(jnp.concatenate([panel[(SHARDS - 1) * SHARD :], spare]))
    arrived = [lax.ppermute(shards[k], axis, SCATTER[k]) for k in range(SHARDS)]
    keeps = jnp.logical_or(index == HOLDER[0][0], index == HOLDER[2][0])
    return jnp.where(keeps, shards[0], sum(arrived[1:], arrived[0]))


def kernel(ints, *refs):
    a_refs, b_refs = refs[: 2 * RING], refs[2 * RING : 2 * RING + 6]
    out, a_all, b_all, a_sp, b_sp, result, lists, sems, list_sems, out_sems = refs[2 * RING + 6 :]
    col, row = ints[51], ints[52]
    x, z = lax.div(col, 2), lax.rem(col, 2)
    y, core = lax.rem(lax.div(row, 2), RING), lax.rem(row, 2)

    copies = []

    def place(ref, part, dest, origin):
        slot = ints[53 + origin]
        copy = pltpu.make_async_copy(
            ref.at[pl.ds(part * SHARD, SHARD), :],
            dest.at[pl.ds(pl.multiple_of(slot * SHARD, SHARD), SHARD), :],
            sems.at[len(copies)],
        )
        copy.start()
        copies.append(copy)

    for half in range(2):
        core_of = core if half == 0 else 1 - core
        way = 1 - 2 * core_of
        for ref, first, count in zip(b_refs[3 * half : 3 * half + 3], (-4, -1, 2), (3, 3, 2)):
            for part in range(count):
                origin_y = lax.rem(y + way * (first + part) + 2 * RING, RING)
                place(ref, part, b_all, origin_y * PAIR + core_of)
    for hop in range(RING):
        origin_x = lax.rem(x - (1 - 2 * core) * hop + RING, RING)
        place(a_refs[hop], 0, a_all, origin_x * PAIR + z)
        place(a_refs[RING + hop], 0, a_all, origin_x * PAIR + (1 - z))

    def split(source, which, dest, order):
        for copy in copies[which * 2 * RING : (which + 1) * 2 * RING]:
            copy.wait()
        asked = []
        for s in range(STEPS):
            copy = pltpu.make_async_copy(
                source.at[pl.ds(s * PANEL + LIST_ROW, 8), pl.ds(0, 128)],
                lists.at[which * STEPS + s],
                list_sems.at[which * STEPS + s],
            )
            copy.start()
            asked.append(copy)
        for s in range(STEPS):
            for t in range(SLOTS):
                value = source[pl.ds(s * PANEL + t * SIDE, SIDE), :]
                high = value.astype(jnp.bfloat16)
                low = (value - high.astype(jnp.float32)).astype(jnp.bfloat16)
                for part, kind in enumerate(order):
                    piece = low if kind else high
                    if which == 0:
                        dest[s * SLOTS + t, :, part * SIDE : (part + 1) * SIDE] = piece
                    else:
                        dest[s * SLOTS + t, part * SIDE : (part + 1) * SIDE, :] = piece
        return asked

    asked = split(b_all, 1, b_sp, (0, 1, 0)) + split(a_all, 0, a_sp, (0, 0, 1))
    for copy in asked:
        copy.wait()

    done = []
    for l in range(RESULTS):
        c_row, c_col = ints[2 * l], ints[2 * l + 1]
        total = None
        for s in range(STEPS):
            i, j = jnp.int32(0), jnp.int32(0)
            for t in range(SLOTS):
                i = jnp.where(lists[s, 0, t].astype(jnp.int32) == c_row, t, i)
                j = jnp.where(lists[STEPS + s, 0, t].astype(jnp.int32) == c_col, t, j)
            live = jnp.int32(0)
            for p in range(RESULTS):
                at = 12 + (s * RESULTS + p) * 2
                hit = (ints[at] == i) & (ints[at + 1] == j) & (p < ints[48 + s])
                live = jnp.where(hit, 1, live)
            product = jnp.dot(
                a_sp[s * SLOTS + i], b_sp[s * SLOTS + j], preferred_element_type=jnp.float32
            )
            product = product * live.astype(jnp.float32)
            total = product if total is None else total + product
        result[l] = total
        copy = pltpu.make_async_copy(result.at[l], out.at[l], out_sems.at[l])
        copy.start()
        done.append(copy)
    for copy in done:
        copy.wait()


def multiply(ints, a_blocks, b_blocks):
    anywhere = pl.BlockSpec(memory_space=pl.ANY)
    count = len(a_blocks) + len(b_blocks)
    rows = (STEPS * SHARDS + 1) * SHARD
    tiles = STEPS * SLOTS
    return pl.pallas_call(
        kernel,
        out_shape=jax.ShapeDtypeStruct((RESULTS, SIDE, SIDE), jnp.float32),
        in_specs=[pl.BlockSpec(memory_space=pltpu.SMEM)] + [anywhere] * count,
        out_specs=anywhere,
        scratch_shapes=[
            pltpu.VMEM((rows, SIDE), jnp.float32),
            pltpu.VMEM((rows, SIDE), jnp.float32),
            pltpu.VMEM((tiles, SIDE, 3 * SIDE), jnp.bfloat16),
            pltpu.VMEM((tiles, 3 * SIDE, SIDE), jnp.bfloat16),
            pltpu.VMEM((RESULTS, SIDE, SIDE), jnp.float32),
            pltpu.SMEM((2 * STEPS, 8, 128), jnp.float32),
            pltpu.SemaphoreType.DMA((4 * RING,)),
            pltpu.SemaphoreType.DMA((2 * STEPS,)),
            pltpu.SemaphoreType.DMA((RESULTS,)),
        ],
        compiler_params=pltpu.CompilerParams(vmem_limit_bytes=20 << 20),
    )(ints, *a_blocks, *b_blocks)


def program(a_tiles, b_tiles, a_rows, b_cols, c_shape, pairs, pair_count):
    col, row = lax.axis_index("col"), lax.axis_index("row")
    ints = jnp.concatenate(
        [
            c_shape.reshape(-1),
            pairs.reshape(-1),
            pair_count.reshape(-1),
            col.astype(jnp.int32)[None],
            row.astype(jnp.int32)[None],
            jnp.array(SLOT_OF, jnp.int32),
        ]
    )

    b_first = scatter(b_tiles[0, 0], b_cols[0, 0], "row", row)
    b_first, ints = lax.optimization_barrier((b_first, ints))
    a_own = scatter(a_tiles[0, 0], a_rows[0, 0], "col", col)
    b_own = b_first + sum(lax.ppermute(b_first, "row", to_plane(z)) for z in range(1, PLANES))

    near_a, far_a = [a_own], [lax.ppermute(a_own, "col", SWAP_Z)]
    for _ in range(1, RING):
        near_a.append(lax.ppermute(near_a[-1], ("row", "col"), ring_x()))
        far_a.append(lax.ppermute(far_a[-1], ("row", "col"), ring_x()))

    behind = lax.ppermute(b_own, "row", ring_y(1))
    ahead = lax.ppermute(b_own, "row", ring_y(-1))
    near = jnp.concatenate([behind, b_own, ahead])
    back = lax.ppermute(near, "row", ring_y(3))
    front = lax.ppermute(near[SHARD:], "row", ring_y(-2))
    mine = [back, near, front]
    other = [lax.ppermute(part, "row", SWAP_CORE) for part in mine]

    return multiply(ints, near_a + far_a, mine + other)[None, None]


def solution(mesh):
    return jax.shard_map(
        program,
        mesh=mesh,
        in_specs=(
            P("row", "col", None, None, None),
            P("row", "col", None, None, None),
            P("row", "col", None),
            P("row", "col", None),
            P("row", "col", None, None),
            P("row", "col", None, None, None),
            P("row", "col", None),
        ),
        out_specs=P("row", "col", None, None, None),
        check_vma=False,
    )
```

```python
import jax
import jax.numpy as jnp
from jax import lax
from jax.experimental import pallas as pl
from jax.experimental.pallas import tpu as pltpu
from jax.sharding import PartitionSpec as P


STEPS, SLOTS, SIDE, RESULTS = 3, 3, 256, 6
RING, PAIR, PLANES = 8, 2, 4
SHARD = 160
SHARDS = 5
PANEL = SHARD * SHARDS
LIST_ROW = SLOTS * SIDE

HOLDERS = (
    ((0, 0), (0, 1), (7, 0), (6, 0), (5, 0)),
    ((6, 1), (7, 1), (2, 1), (3, 1), (4, 1)),
    ((1, 0), (1, 1), (2, 0), (3, 0), (4, 0)),
)
HOLDER = tuple(tuple(ring * PAIR + pair for ring, pair in panel) for panel in HOLDERS)
SLOT_OF = [STEPS * SHARDS] * (RING * PAIR)
for _s in range(STEPS):
    for _k in range(SHARDS):
        SLOT_OF[HOLDER[_s][_k]] = _s * SHARDS + _k

SCATTER = [
    [(s, HOLDER[s][k]) for s in range(STEPS) if HOLDER[s][k] != s] for k in range(SHARDS)
]


def ring_x(step):
    columns = RING * PAIR
    pairs = []
    for r in range(PLANES * RING * PAIR):
        for c in range(columns):
            to = (c + PAIR * (step if r % PAIR == 0 else -step)) % columns
            pairs.append((r * columns + c, r * columns + to))
    return pairs


def ring_y(step):
    pairs = []
    for z in range(PLANES):
        for y in range(RING):
            for core in range(PAIR):
                to = (y + (step if core == 0 else -step)) % RING
                pairs.append(((z * RING + y) * PAIR + core, (z * RING + to) * PAIR + core))
    return pairs


SWAP_Z = [(c, c ^ 1) for c in range(RING * PAIR)]
SWAP_CORE = [(r, r ^ 1) for r in range(PLANES * RING * PAIR)]


def to_plane(z):
    return [(r, z * RING * PAIR + r) for r in range(RING * PAIR)]


def scatter(tiles, listed, axis, index):
    panel = tiles.reshape(SLOTS * SIDE, SIDE)
    spare = jnp.pad(listed.astype(jnp.float32)[None, :], ((0, PANEL - LIST_ROW - 1), (0, SIDE - SLOTS)))
    shards = [panel[k * SHARD : (k + 1) * SHARD] for k in range(SHARDS - 1)]
    shards.append(jnp.concatenate([panel[(SHARDS - 1) * SHARD :], spare]))
    arrived = [lax.ppermute(shards[k], axis, SCATTER[k]) for k in range(SHARDS)]
    keeps = jnp.logical_or(index == HOLDER[0][0], index == HOLDER[2][0])
    return jnp.where(keeps, shards[0], sum(arrived[1:], arrived[0]))


def kernel(ints, *refs):
    a_refs, b_refs = refs[:RING], refs[RING : RING + 6]
    out, a_sp, b_sp, lists, list_sems = refs[RING + 6 :]
    col, row = ints[51], ints[52]
    x, z = lax.div(col, 2), lax.rem(col, 2)
    y, core = lax.rem(lax.div(row, 2), RING), lax.rem(row, 2)

    places = []
    for half in range(2):
        core_of = core if half == 0 else 1 - core
        way = 1 - 2 * core_of
        for ref, first, count in zip(b_refs[3 * half : 3 * half + 3], (-4, -1, 2), (3, 3, 2)):
            for part in range(count):
                origin_y = lax.rem(y + way * (first + part) + 2 * RING, RING)
                places.append((ref, part, b_sp, origin_y * PAIR + core_of))
    way = 1 - 2 * core
    for ref, shift in zip(a_refs, (0, -1, 1, -2, 2, -3, 3, -4)):
        origin_x = lax.rem(x + way * shift + RING, RING)
        places.append((ref, 0, a_sp, origin_x * PAIR + z))
        places.append((ref, 1, a_sp, origin_x * PAIR + (1 - z)))

    asked = []
    for n, (ref, part, dest, origin) in enumerate(places):
        slot = ints[53 + origin] + (0 if dest is a_sp else 2 * RING)
        copy = pltpu.make_async_copy(
            ref.at[pl.ds(part * SHARD + LIST_ROW % SHARD, 8), pl.ds(0, 128)],
            lists.at[slot],
            list_sems.at[n],
        )
        copy.start()
        asked.append(copy)
    for ref, part, dest, origin in places:
        slot = ints[53 + origin]
        value = ref[part * SHARD : (part + 1) * SHARD, :]
        high = value.astype(jnp.bfloat16)
        low = (value - high.astype(jnp.float32)).astype(jnp.bfloat16)
        at = pl.ds(pl.multiple_of(slot * SHARD, SHARD), SHARD)
        dest[at, :SIDE] = high
        dest[at, SIDE:] = low
    for copy in asked:
        copy.wait()

    for l in range(RESULTS):
        c_row, c_col = ints[2 * l], ints[2 * l + 1]
        total = None
        for s in range(STEPS):
            last = s * SHARDS + SHARDS - 1
            i, j = jnp.int32(0), jnp.int32(0)
            for t in range(SLOTS):
                i = jnp.where(lists[last, 0, t].astype(jnp.int32) == c_row, t, i)
                j = jnp.where(lists[2 * RING + last, 0, t].astype(jnp.int32) == c_col, t, j)
            live = jnp.int32(0)
            for p in range(RESULTS):
                at = 12 + (s * RESULTS + p) * 2
                hit = (ints[at] == i) & (ints[at + 1] == j) & (p < ints[48 + s])
                live = jnp.where(hit, 1, live)
            ia = pl.ds(pl.multiple_of(s * PANEL + i * SIDE, 32), SIDE)
            jb = pl.ds(pl.multiple_of(s * PANEL + j * SIDE, 32), SIDE)
            product = (
                jnp.dot(a_sp[ia, :SIDE], b_sp[jb, :SIDE], preferred_element_type=jnp.float32)
                + jnp.dot(a_sp[ia, :SIDE], b_sp[jb, SIDE:], preferred_element_type=jnp.float32)
                + jnp.dot(a_sp[ia, SIDE:], b_sp[jb, :SIDE], preferred_element_type=jnp.float32)
            )
            product = product * live.astype(jnp.float32)
            total = product if total is None else total + product
        out[l] = total


def multiply(ints, a_blocks, b_blocks):
    local = pl.BlockSpec(memory_space=pltpu.VMEM)
    count = len(a_blocks) + len(b_blocks)
    rows = (STEPS * SHARDS + 1) * SHARD
    return pl.pallas_call(
        kernel,
        out_shape=jax.ShapeDtypeStruct((RESULTS, SIDE, SIDE), jnp.float32),
        in_specs=[pl.BlockSpec(memory_space=pltpu.SMEM)] + [local] * count,
        out_specs=local,
        scratch_shapes=[
            pltpu.VMEM((rows, 2 * SIDE), jnp.bfloat16),
            pltpu.VMEM((rows, 2 * SIDE), jnp.bfloat16),
            pltpu.SMEM((4 * RING, 8, 128), jnp.float32),
            pltpu.SemaphoreType.DMA((4 * RING,)),
        ],
        compiler_params=pltpu.CompilerParams(vmem_limit_bytes=24 << 20),
    )(ints, *a_blocks, *b_blocks)


def program(a_tiles, b_tiles, a_rows, b_cols, c_shape, pairs, pair_count):
    col, row = lax.axis_index("col"), lax.axis_index("row")
    ints = jnp.concatenate(
        [
            c_shape.reshape(-1),
            pairs.reshape(-1),
            pair_count.reshape(-1),
            col.astype(jnp.int32)[None],
            row.astype(jnp.int32)[None],
            jnp.array(SLOT_OF, jnp.int32),
        ]
    )

    a_own = scatter(a_tiles[0, 0], a_rows[0, 0], "col", col)
    b_first = scatter(b_tiles[0, 0], b_cols[0, 0], "row", row)
    b_first, ints = lax.optimization_barrier((b_first, ints))
    b_own = b_first + sum(lax.ppermute(b_first, "row", to_plane(z)) for z in range(1, PLANES))

    block = jnp.concatenate([a_own, lax.ppermute(a_own, "col", SWAP_Z)])
    a_blocks, after, before = [block], block, block
    for _ in range(1, RING // 2):
        after = lax.ppermute(after, ("row", "col"), ring_x(1))
        before = lax.ppermute(before, ("row", "col"), ring_x(-1))
        a_blocks += [after, before]
    a_blocks.append(lax.ppermute(after, ("row", "col"), ring_x(1)))

    behind = lax.ppermute(b_own, "row", ring_y(1))
    ahead = lax.ppermute(b_own, "row", ring_y(-1))
    near = jnp.concatenate([behind, b_own, ahead])
    back = lax.ppermute(near, "row", ring_y(3))
    front = lax.ppermute(near[SHARD:], "row", ring_y(-2))
    mine = [back, near, front]
    other = [lax.ppermute(part, "row", SWAP_CORE) for part in mine]

    return multiply(ints, a_blocks, mine + other)[None, None]


def solution(mesh):
    return jax.shard_map(
        program,
        mesh=mesh,
        in_specs=(
            P("row", "col", None, None, None),
            P("row", "col", None, None, None),
            P("row", "col", None),
            P("row", "col", None),
            P("row", "col", None, None),
            P("row", "col", None, None, None),
            P("row", "col", None),
        ),
        out_specs=P("row", "col", None, None, None),
        check_vma=False,
    )
```

```python
import jax
import jax.numpy as jnp
from jax import lax
from jax.experimental import pallas as pl
from jax.experimental.pallas import tpu as pltpu
from jax.sharding import PartitionSpec as P


STEPS, SLOTS, SIDE, RESULTS = 3, 3, 256, 6
RING, PAIR, PLANES = 8, 2, 4
SHARD = 160
SHARDS = 5
PANEL = SLOTS * SIDE
LIST = SHARDS * SHARD - PANEL

HOLDERS = (
    ((0, 0), (0, 1), (7, 0), (6, 0), (5, 0)),
    ((6, 1), (7, 1), (2, 1), (3, 1), (4, 1)),
    ((1, 0), (1, 1), (2, 0), (3, 0), (4, 0)),
)
HOLDER = tuple(tuple(ring * PAIR + pair for ring, pair in panel) for panel in HOLDERS)
HEAD_AT = [STEPS * PANEL] * (RING * PAIR)
REST_AT = [STEPS * PANEL + LIST] * (RING * PAIR)
for _s in range(STEPS):
    for _k in range(SHARDS):
        _at = _s * PANEL + min(_k * SHARD, PANEL - SHARD)
        REST_AT[HOLDER[_s][_k]] = _at + LIST
        if _k < SHARDS - 1:
            HEAD_AT[HOLDER[_s][_k]] = _at

SCATTER = [
    [(s, HOLDER[s][k]) for s in range(STEPS) if HOLDER[s][k] != s] for k in range(SHARDS)
]


def ring_x(step):
    columns = RING * PAIR
    pairs = []
    for r in range(PLANES * RING * PAIR):
        for c in range(columns):
            to = (c + PAIR * (step if r % PAIR == 0 else -step)) % columns
            pairs.append((r * columns + c, r * columns + to))
    return pairs


def ring_y(step):
    pairs = []
    for z in range(PLANES):
        for y in range(RING):
            for core in range(PAIR):
                to = (y + (step if core == 0 else -step)) % RING
                pairs.append(((z * RING + y) * PAIR + core, (z * RING + to) * PAIR + core))
    return pairs


SWAP_Z = [(c, c ^ 1) for c in range(RING * PAIR)]
SWAP_CORE = [(r, r ^ 1) for r in range(PLANES * RING * PAIR)]


def to_plane(z):
    return [(r, z * RING * PAIR + r) for r in range(RING * PAIR)]


def scatter(tiles, listed, axis, index):
    panel = tiles.reshape(SLOTS * SIDE, SIDE)
    shards = [panel[k * SHARD : (k + 1) * SHARD] for k in range(SHARDS - 1)]
    spare = jnp.pad(listed[None, :], ((0, SHARD - 1), (0, SIDE - SLOTS))).astype(jnp.float32)
    rows = lax.broadcasted_iota(jnp.int32, (SHARD, SIDE), 0)
    shards.append(jnp.where(rows < LIST, spare, panel[PANEL - SHARD :]))
    arrived = [lax.ppermute(shards[k], axis, SCATTER[k]) for k in range(SHARDS)]
    keeps = jnp.logical_or(index == HOLDER[0][0], index == HOLDER[2][0])
    return jnp.where(keeps, shards[0], sum(arrived[1:], arrived[0]))


def kernel(ints, *refs):
    a_refs, b_refs = refs[:RING], refs[RING : RING + 6]
    out, a_sp, b_sp, lists, list_sems = refs[RING + 6 :]
    col, row = ints[51], ints[52]
    x, z = lax.div(col, 2), lax.rem(col, 2)
    y, core = lax.rem(lax.div(row, 2), RING), lax.rem(row, 2)

    places = []
    for half in range(2):
        core_of = core if half == 0 else 1 - core
        way = 1 - 2 * core_of
        for ref, first, count in zip(b_refs[3 * half : 3 * half + 3], (-4, -1, 2), (3, 3, 2)):
            for part in range(count):
                origin_y = lax.rem(y + way * (first + part) + 2 * RING, RING)
                places.append((ref, part, b_sp, origin_y * PAIR + core_of))
    way = 1 - 2 * core
    for ref, shift in zip(a_refs, (0, -1, 1, -2, 2, -3, 3, -4)):
        origin_x = lax.rem(x + way * shift + RING, RING)
        places.append((ref, 0, a_sp, origin_x * PAIR + z))
        places.append((ref, 1, a_sp, origin_x * PAIR + (1 - z)))

    asked = []
    for n, (ref, part, dest, origin) in enumerate(places):
        copy = pltpu.make_async_copy(
            ref.at[pl.ds(part * SHARD, 8), pl.ds(0, 128)],
            lists.at[origin + (0 if dest is a_sp else 2 * RING)],
            list_sems.at[n],
        )
        copy.start()
        asked.append(copy)
    for ref, part, dest, origin in places:
        value = ref[part * SHARD : (part + 1) * SHARD, :]
        high = value.astype(jnp.bfloat16)
        low = (value - high.astype(jnp.float32)).astype(jnp.bfloat16)
        head = pl.ds(pl.multiple_of(ints[53 + origin], LIST), LIST)
        rest = pl.ds(pl.multiple_of(ints[53 + 2 * RING + origin], LIST), SHARD - LIST)
        dest[head, :SIDE] = high[:LIST]
        dest[head, SIDE:] = low[:LIST]
        dest[rest, :SIDE] = high[LIST:]
        dest[rest, SIDE:] = low[LIST:]
    for copy in asked:
        copy.wait()

    for l in range(RESULTS):
        c_row, c_col = ints[2 * l], ints[2 * l + 1]
        total = None
        for s in range(STEPS):
            last = HOLDER[s][SHARDS - 1]
            i, j = jnp.int32(0), jnp.int32(0)
            for t in range(SLOTS):
                i = jnp.where(lists[last, 0, t].astype(jnp.int32) == c_row, t, i)
                j = jnp.where(lists[2 * RING + last, 0, t].astype(jnp.int32) == c_col, t, j)
            live = jnp.int32(0)
            for p in range(RESULTS):
                at = 12 + (s * RESULTS + p) * 2
                hit = (ints[at] == i) & (ints[at + 1] == j) & (p < ints[48 + s])
                live = jnp.where(hit, 1, live)
            ia = pl.ds(pl.multiple_of(s * PANEL + i * SIDE, 32), SIDE)
            jb = pl.ds(pl.multiple_of(s * PANEL + j * SIDE, 32), SIDE)
            product = (
                jnp.dot(a_sp[ia, :SIDE], b_sp[jb, :SIDE], preferred_element_type=jnp.float32)
                + jnp.dot(a_sp[ia, :SIDE], b_sp[jb, SIDE:], preferred_element_type=jnp.float32)
                + jnp.dot(a_sp[ia, SIDE:], b_sp[jb, :SIDE], preferred_element_type=jnp.float32)
            )
            product = product * live.astype(jnp.float32)
            total = product if total is None else total + product
        out[l] = total


def multiply(ints, a_blocks, b_blocks):
    local = pl.BlockSpec(memory_space=pltpu.VMEM)
    count = len(a_blocks) + len(b_blocks)
    rows = STEPS * PANEL + SHARD
    return pl.pallas_call(
        kernel,
        out_shape=jax.ShapeDtypeStruct((RESULTS, SIDE, SIDE), jnp.float32),
        in_specs=[pl.BlockSpec(memory_space=pltpu.SMEM)] + [local] * count,
        out_specs=local,
        scratch_shapes=[
            pltpu.VMEM((rows, 2 * SIDE), jnp.bfloat16),
            pltpu.VMEM((rows, 2 * SIDE), jnp.bfloat16),
            pltpu.SMEM((4 * RING, 8, 128), jnp.float32),
            pltpu.SemaphoreType.DMA((4 * RING,)),
        ],
        compiler_params=pltpu.CompilerParams(vmem_limit_bytes=24 << 20),
    )(ints, *a_blocks, *b_blocks)


def program(a_tiles, b_tiles, a_rows, b_cols, c_shape, pairs, pair_count):
    col, row = lax.axis_index("col"), lax.axis_index("row")
    ints = jnp.concatenate(
        [
            c_shape.reshape(-1),
            pairs.reshape(-1),
            pair_count.reshape(-1),
            col.astype(jnp.int32)[None],
            row.astype(jnp.int32)[None],
            jnp.array(HEAD_AT + REST_AT, jnp.int32),
        ]
    )

    a_own = scatter(a_tiles[0, 0], a_rows[0, 0], "col", col)
    b_first = scatter(b_tiles[0, 0], b_cols[0, 0], "row", row)
    b_first, ints = lax.optimization_barrier((b_first, ints))
    b_own = b_first + sum(lax.ppermute(b_first, "row", to_plane(z)) for z in range(1, PLANES))

    block = jnp.concatenate([a_own, lax.ppermute(a_own, "col", SWAP_Z)])
    a_blocks, after, before = [block], block, block
    for _ in range(1, RING // 2):
        after = lax.ppermute(after, ("row", "col"), ring_x(1))
        before = lax.ppermute(before, ("row", "col"), ring_x(-1))
        a_blocks += [after, before]
    a_blocks.append(lax.ppermute(after, ("row", "col"), ring_x(1)))

    behind = lax.ppermute(b_own, "row", ring_y(1))
    ahead = lax.ppermute(b_own, "row", ring_y(-1))
    near = jnp.concatenate([behind, b_own, ahead])
    back = lax.ppermute(near, "row", ring_y(3))
    front = lax.ppermute(near[SHARD:], "row", ring_y(-2))
    mine = [back, near, front]
    other = [lax.ppermute(part, "row", SWAP_CORE) for part in mine]

    return multiply(ints, a_blocks, mine + other)[None, None]


def solution(mesh):
    return jax.shard_map(
        program,
        mesh=mesh,
        in_specs=(
            P("row", "col", None, None, None),
            P("row", "col", None, None, None),
            P("row", "col", None),
            P("row", "col", None),
            P("row", "col", None, None),
            P("row", "col", None, None, None),
            P("row", "col", None),
        ),
        out_specs=P("row", "col", None, None, None),
        check_vma=False,
    )
```

```python
import jax
import jax.numpy as jnp
from jax import lax
from jax.experimental import pallas as pl
from jax.experimental.pallas import tpu as pltpu
from jax.sharding import PartitionSpec as P


STEPS, SLOTS, SIDE, RESULTS = 3, 3, 256, 6
RING, PAIR, PLANES = 8, 2, 4
SHARD = 160
SHARDS = 5
PANEL = SLOTS * SIDE
LIST = SHARDS * SHARD - PANEL

HOLDERS = (
    ((0, 0), (0, 1), (7, 0), (6, 0), (5, 0)),
    ((7, 1), (6, 1), (2, 1), (3, 1), (4, 1)),
    ((1, 0), (1, 1), (2, 0), (3, 0), (4, 0)),
)
HOLDER = tuple(tuple(ring * PAIR + pair for ring, pair in panel) for panel in HOLDERS)
HEAD_AT = [STEPS * PANEL] * (RING * PAIR)
REST_AT = [STEPS * PANEL + LIST] * (RING * PAIR)
for _s in range(STEPS):
    for _k in range(SHARDS):
        _at = _s * PANEL + min(_k * SHARD, PANEL - SHARD)
        REST_AT[HOLDER[_s][_k]] = _at + LIST
        if _k < SHARDS - 1:
            HEAD_AT[HOLDER[_s][_k]] = _at

SCATTER = [
    [(s, HOLDER[s][k]) for s in range(STEPS) if HOLDER[s][k] != s] for k in range(SHARDS)
]


def ring_x(step):
    columns = RING * PAIR
    pairs = []
    for r in range(PLANES * RING * PAIR):
        for c in range(columns):
            to = (c + PAIR * (step if r % PAIR == 0 else -step)) % columns
            pairs.append((r * columns + c, r * columns + to))
    return pairs


def ring_y(step):
    pairs = []
    for z in range(PLANES):
        for y in range(RING):
            for core in range(PAIR):
                to = (y + (step if core == 0 else -step)) % RING
                pairs.append(((z * RING + y) * PAIR + core, (z * RING + to) * PAIR + core))
    return pairs


SWAP_Z = [(c, c ^ 1) for c in range(RING * PAIR)]
SWAP_CORE = [(r, r ^ 1) for r in range(PLANES * RING * PAIR)]


def to_plane(z):
    return [(r, z * RING * PAIR + r) for r in range(RING * PAIR)]


def scatter(tiles, listed, axis, index):
    panel = tiles.reshape(SLOTS * SIDE, SIDE)
    shards = [panel[k * SHARD : (k + 1) * SHARD] for k in range(SHARDS - 1)]
    spare = jnp.pad(listed[None, :], ((0, SHARD - 1), (0, SIDE - SLOTS))).astype(jnp.float32)
    rows = lax.broadcasted_iota(jnp.int32, (SHARD, SIDE), 0)
    shards.append(jnp.where(rows < LIST, spare, panel[PANEL - SHARD :]))
    arrived = [lax.ppermute(shards[k], axis, SCATTER[k]) for k in range(SHARDS)]
    keeps = jnp.logical_or(index == HOLDER[0][0], index == HOLDER[2][0])
    return jnp.where(keeps, shards[0], sum(arrived[1:], arrived[0]))


EARLY_A, EARLY_B = 5, (1, 4)


def placements(ints, a_refs, b_refs, a_sp, b_sp):
    col, row = ints[51], ints[52]
    x, z = lax.div(col, 2), lax.rem(col, 2)
    y, core = lax.rem(lax.div(row, 2), RING), lax.rem(row, 2)
    places = []
    for half in range(2):
        core_of = core if half == 0 else 1 - core
        way = 1 - 2 * core_of
        for i, (first, count) in enumerate(zip((-4, -1, 2), (3, 3, 2))):
            at = 3 * half + i
            for part in range(count):
                origin_y = lax.rem(y + way * (first + part) + 2 * RING, RING)
                places.append((b_refs[at], part, b_sp, origin_y * PAIR + core_of, at in EARLY_B))
    way = 1 - 2 * core
    for i, shift in enumerate((0, -1, 1, -2, 2, -3, 3, -4)):
        origin_x = lax.rem(x + way * shift + RING, RING)
        places.append((a_refs[i], 0, a_sp, origin_x * PAIR + z, i < EARLY_A))
        places.append((a_refs[i], 1, a_sp, origin_x * PAIR + (1 - z), i < EARLY_A))
    return places


def split(ints, places):
    for ref, part, dest, origin, _ in places:
        value = ref[part * SHARD : (part + 1) * SHARD, :]
        high = value.astype(jnp.bfloat16)
        low = (value - high.astype(jnp.float32)).astype(jnp.bfloat16)
        head = pl.ds(pl.multiple_of(ints[53 + origin], LIST), LIST)
        rest = pl.ds(pl.multiple_of(ints[53 + 2 * RING + origin], LIST), SHARD - LIST)
        dest[head, :SIDE] = high[:LIST]
        dest[head, SIDE:] = low[:LIST]
        dest[rest, :SIDE] = high[LIST:]
        dest[rest, SIDE:] = low[LIST:]


def early_kernel(ints, *refs):
    a_refs = list(refs[:EARLY_A]) + [None] * (RING - EARLY_A)
    b_refs = [None] * 6
    for at, ref in zip(EARLY_B, refs[EARLY_A : EARLY_A + len(EARLY_B)]):
        b_refs[at] = ref
    places = placements(ints, a_refs, b_refs, *refs[EARLY_A + len(EARLY_B) :])
    split(ints, [place for place in places if place[4]])


def kernel(ints, *refs):
    a_refs, b_refs = refs[:RING], refs[RING : RING + 6]
    out, a_sp, b_sp, lists, list_sems = refs[RING + 8 :]
    places = placements(ints, a_refs, b_refs, a_sp, b_sp)

    asked = []
    for n, (ref, part, dest, origin, _) in enumerate(places):
        copy = pltpu.make_async_copy(
            ref.at[pl.ds(part * SHARD, 8), pl.ds(0, 128)],
            lists.at[origin + (0 if dest is a_sp else 2 * RING)],
            list_sems.at[n],
        )
        copy.start()
        asked.append(copy)
    split(ints, [place for place in places if not place[4]])
    for copy in asked:
        copy.wait()

    for l in range(RESULTS):
        c_row, c_col = ints[2 * l], ints[2 * l + 1]
        total = None
        for s in range(STEPS):
            last = HOLDER[s][SHARDS - 1]
            i, j = jnp.int32(0), jnp.int32(0)
            for t in range(SLOTS):
                i = jnp.where(lists[last, 0, t].astype(jnp.int32) == c_row, t, i)
                j = jnp.where(lists[2 * RING + last, 0, t].astype(jnp.int32) == c_col, t, j)
            live = jnp.int32(0)
            for p in range(RESULTS):
                at = 12 + (s * RESULTS + p) * 2
                hit = (ints[at] == i) & (ints[at + 1] == j) & (p < ints[48 + s])
                live = jnp.where(hit, 1, live)
            ia = pl.ds(pl.multiple_of(s * PANEL + i * SIDE, 32), SIDE)
            jb = pl.ds(pl.multiple_of(s * PANEL + j * SIDE, 32), SIDE)
            product = (
                jnp.dot(a_sp[ia, :SIDE], b_sp[jb, :SIDE], preferred_element_type=jnp.float32)
                + jnp.dot(a_sp[ia, :SIDE], b_sp[jb, SIDE:], preferred_element_type=jnp.float32)
                + jnp.dot(a_sp[ia, SIDE:], b_sp[jb, :SIDE], preferred_element_type=jnp.float32)
            )
            product = product * live.astype(jnp.float32)
            total = product if total is None else total + product
        out[l] = total


def multiply(ints, a_blocks, b_blocks):
    local = pl.BlockSpec(memory_space=pltpu.VMEM)
    scalars = pl.BlockSpec(memory_space=pltpu.SMEM)
    halves = jax.ShapeDtypeStruct((STEPS * PANEL + SHARD, 2 * SIDE), jnp.bfloat16)
    early = list(a_blocks[:EARLY_A]) + [b_blocks[at] for at in EARLY_B]
    a_sp, b_sp = pl.pallas_call(
        early_kernel,
        out_shape=(halves, halves),
        in_specs=[scalars] + [local] * len(early),
        out_specs=(local, local),
        compiler_params=pltpu.CompilerParams(vmem_limit_bytes=24 << 20),
        name="early",
    )(ints, *early)
    count = len(a_blocks) + len(b_blocks)
    return pl.pallas_call(
        kernel,
        out_shape=(jax.ShapeDtypeStruct((RESULTS, SIDE, SIDE), jnp.float32), halves, halves),
        in_specs=[scalars] + [local] * (count + 2),
        out_specs=(local, local, local),
        input_output_aliases={count + 1: 1, count + 2: 2},
        scratch_shapes=[
            pltpu.SMEM((4 * RING, 8, 128), jnp.float32),
            pltpu.SemaphoreType.DMA((4 * RING,)),
        ],
        compiler_params=pltpu.CompilerParams(vmem_limit_bytes=24 << 20),
        name="multiply",
    )(ints, *a_blocks, *b_blocks, a_sp, b_sp)[0]


def program(a_tiles, b_tiles, a_rows, b_cols, c_shape, pairs, pair_count):
    col, row = lax.axis_index("col"), lax.axis_index("row")
    ints = jnp.concatenate(
        [
            c_shape.reshape(-1),
            pairs.reshape(-1),
            pair_count.reshape(-1),
            col.astype(jnp.int32)[None],
            row.astype(jnp.int32)[None],
            jnp.array(HEAD_AT + REST_AT, jnp.int32),
        ]
    )

    a_own = scatter(a_tiles[0, 0], a_rows[0, 0], "col", col)
    b_first = scatter(b_tiles[0, 0], b_cols[0, 0], "row", row)
    b_first, ints = lax.optimization_barrier((b_first, ints))
    b_own = b_first + sum(lax.ppermute(b_first, "row", to_plane(z)) for z in range(1, PLANES))

    block = jnp.concatenate([a_own, lax.ppermute(a_own, "col", SWAP_Z)])
    a_blocks, after, before = [block], block, block
    for _ in range(1, RING // 2):
        after = lax.ppermute(after, ("row", "col"), ring_x(1))
        before = lax.ppermute(before, ("row", "col"), ring_x(-1))
        a_blocks += [after, before]
    a_blocks.append(lax.ppermute(after, ("row", "col"), ring_x(1)))

    behind = lax.ppermute(b_own, "row", ring_y(1))
    ahead = lax.ppermute(b_own, "row", ring_y(-1))
    near = jnp.concatenate([behind, b_own, ahead])
    back = lax.ppermute(near, "row", ring_y(3))
    front = lax.ppermute(near[SHARD:], "row", ring_y(-2))
    mine = [back, near, front]
    other = [lax.ppermute(part, "row", SWAP_CORE) for part in mine]

    return multiply(ints, a_blocks, mine + other)[None, None]


def solution(mesh):
    return jax.shard_map(
        program,
        mesh=mesh,
        in_specs=(
            P("row", "col", None, None, None),
            P("row", "col", None, None, None),
            P("row", "col", None),
            P("row", "col", None),
            P("row", "col", None, None),
            P("row", "col", None, None, None),
            P("row", "col", None),
        ),
        out_specs=P("row", "col", None, None, None),
        check_vma=False,
    )
```

```python
import jax
import jax.numpy as jnp
from jax import lax
from jax.experimental import pallas as pl
from jax.experimental.pallas import tpu as pltpu
from jax.sharding import PartitionSpec as P


STEPS, SLOTS, SIDE, RESULTS = 3, 3, 256, 6
RING, PAIR, PLANES = 8, 2, 4
SHARD = 160
SHARDS = 5
PANEL = SLOTS * SIDE
LIST = SHARDS * SHARD - PANEL

HOLDERS = (
    ((0, 0), (0, 1), (7, 0), (6, 0), (5, 0)),
    ((7, 1), (6, 1), (2, 1), (3, 1), (4, 1)),
    ((1, 0), (1, 1), (2, 0), (3, 0), (4, 0)),
)
HOLDER = tuple(tuple(ring * PAIR + pair for ring, pair in panel) for panel in HOLDERS)
HEAD_AT = [STEPS * PANEL] * (RING * PAIR)
REST_AT = [STEPS * PANEL + LIST] * (RING * PAIR)
for _s in range(STEPS):
    for _k in range(SHARDS):
        _at = _s * PANEL + min(_k * SHARD, PANEL - SHARD)
        REST_AT[HOLDER[_s][_k]] = _at + LIST
        if _k < SHARDS - 1:
            HEAD_AT[HOLDER[_s][_k]] = _at

SCATTER = [
    [(s, HOLDER[s][k]) for s in range(STEPS) if HOLDER[s][k] != s] for k in range(SHARDS)
]


def ring_x(step):
    columns = RING * PAIR
    pairs = []
    for r in range(PLANES * RING * PAIR):
        for c in range(columns):
            to = (c + PAIR * (step if r % PAIR == 0 else -step)) % columns
            pairs.append((r * columns + c, r * columns + to))
    return pairs


def ring_y(step):
    pairs = []
    for z in range(PLANES):
        for y in range(RING):
            for core in range(PAIR):
                to = (y + (step if core == 0 else -step)) % RING
                pairs.append(((z * RING + y) * PAIR + core, (z * RING + to) * PAIR + core))
    return pairs


SWAP_Z = [(c, c ^ 1) for c in range(RING * PAIR)]
SWAP_CORE = [(r, r ^ 1) for r in range(PLANES * RING * PAIR)]


def to_plane(z):
    return [(r, z * RING * PAIR + r) for r in range(RING * PAIR)]


def scatter(tiles, listed, axis, index):
    panel = tiles.reshape(SLOTS * SIDE, SIDE)
    shards = [panel[k * SHARD : (k + 1) * SHARD] for k in range(SHARDS - 1)]
    spare = jnp.pad(listed[None, :], ((0, SHARD - 1), (0, SIDE - SLOTS))).astype(jnp.float32)
    rows = lax.broadcasted_iota(jnp.int32, (SHARD, SIDE), 0)
    shards.append(jnp.where(rows < LIST, spare, panel[PANEL - SHARD :]))
    arrived = [lax.ppermute(shards[k], axis, SCATTER[k]) for k in range(SHARDS)]
    keeps = jnp.logical_or(index == HOLDER[0][0], index == HOLDER[2][0])
    return jnp.where(keeps, shards[0], sum(arrived[1:], arrived[0]))


EARLY_A, EARLY_B = 5, (1, 4)


def placements(ints, a_refs, b_refs, a_sp, b_sp):
    col, row = ints[51], ints[52]
    x, z = lax.div(col, 2), lax.rem(col, 2)
    y, core = lax.rem(lax.div(row, 2), RING), lax.rem(row, 2)
    places = []
    for half in range(2):
        core_of = core if half == 0 else 1 - core
        way = 1 - 2 * core_of
        for i, (first, count) in enumerate(zip((-4, -1, 2), (3, 3, 2))):
            at = 3 * half + i
            for part in range(count):
                origin_y = lax.rem(y + way * (first + part) + 2 * RING, RING)
                places.append((b_refs[at], part, b_sp, origin_y * PAIR + core_of, at in EARLY_B))
    way = 1 - 2 * core
    for i, shift in enumerate((0, -1, 1, -2, 2, -3, 3, -4)):
        origin_x = lax.rem(x + way * shift + RING, RING)
        places.append((a_refs[i], 0, a_sp, origin_x * PAIR + z, i < EARLY_A))
        places.append((a_refs[i], 1, a_sp, origin_x * PAIR + (1 - z), i < EARLY_A))
    return places


def split(ints, places):
    for ref, part, dest, origin, _ in places:
        value = ref[part * SHARD : (part + 1) * SHARD, :]
        high = value.astype(jnp.bfloat16)
        low = (value - high.astype(jnp.float32)).astype(jnp.bfloat16)
        head = pl.ds(pl.multiple_of(ints[53 + origin], LIST), LIST)
        rest = pl.ds(pl.multiple_of(ints[53 + 2 * RING + origin], LIST), SHARD - LIST)
        dest[head, :SIDE] = high[:LIST]
        dest[head, SIDE:] = low[:LIST]
        dest[rest, :SIDE] = high[LIST:]
        dest[rest, SIDE:] = low[LIST:]


def early_kernel(ints, *refs):
    a_refs = list(refs[:EARLY_A]) + [None] * (RING - EARLY_A)
    b_refs = [None] * 6
    for at, ref in zip(EARLY_B, refs[EARLY_A : EARLY_A + len(EARLY_B)]):
        b_refs[at] = ref
    places = placements(ints, a_refs, b_refs, *refs[EARLY_A + len(EARLY_B) :])
    split(ints, [place for place in places if place[4]])


def kernel(ints, *refs):
    a_refs, b_refs = refs[:RING], refs[RING : RING + 6]
    out, a_sp, b_sp, lists, live, sized, list_sem = refs[RING + 8 :]
    places = placements(ints, a_refs, b_refs, a_sp, b_sp)

    for ref, part, dest, origin, _ in places:
        pltpu.make_async_copy(
            ref.at[pl.ds(part * SHARD, 8), pl.ds(0, 128)],
            lists.at[origin + (0 if dest is a_sp else 2 * RING)],
            list_sem,
        ).start()
    split(ints, [place for place in places if not place[4]])
    for at in range(STEPS * SLOTS * SLOTS):
        live[at] = 0.0
    for s in range(STEPS):
        for p in range(RESULTS):
            at = 12 + (s * RESULTS + p) * 2
            cell = s * SLOTS * SLOTS + ints[at] * SLOTS + ints[at + 1]
            live[cell] = jnp.where(p < ints[48 + s], 1.0, live[cell])

    pltpu.make_async_copy(sized, lists, list_sem).wait()
    known_rows, known_cols = [], []
    for s in range(STEPS):
        last = HOLDER[s][SHARDS - 1]
        known_rows.append([lists[last, 0, t].astype(jnp.int32) for t in range(1, SLOTS)])
        known_cols.append([lists[2 * RING + last, 0, t].astype(jnp.int32) for t in range(1, SLOTS)])

    for l in range(RESULTS):
        c_row, c_col = ints[2 * l], ints[2 * l + 1]
        total = None
        for s in range(STEPS):
            i, j = jnp.int32(0), jnp.int32(0)
            for t in range(1, SLOTS):
                i = jnp.where(known_rows[s][t - 1] == c_row, t, i)
                j = jnp.where(known_cols[s][t - 1] == c_col, t, j)
            weight = live[s * SLOTS * SLOTS + i * SLOTS + j]
            ia = pl.ds(pl.multiple_of(s * PANEL + i * SIDE, 32), SIDE)
            jb = pl.ds(pl.multiple_of(s * PANEL + j * SIDE, 32), SIDE)
            product = (
                jnp.dot(a_sp[ia, :SIDE], b_sp[jb, :SIDE], preferred_element_type=jnp.float32)
                + jnp.dot(a_sp[ia, :SIDE], b_sp[jb, SIDE:], preferred_element_type=jnp.float32)
                + jnp.dot(a_sp[ia, SIDE:], b_sp[jb, :SIDE], preferred_element_type=jnp.float32)
            )
            product = product * weight
            total = product if total is None else total + product
        out[l] = total


def multiply(ints, a_blocks, b_blocks):
    local = pl.BlockSpec(memory_space=pltpu.VMEM)
    scalars = pl.BlockSpec(memory_space=pltpu.SMEM)
    halves = jax.ShapeDtypeStruct((STEPS * PANEL + SHARD, 2 * SIDE), jnp.bfloat16)
    early = list(a_blocks[:EARLY_A]) + [b_blocks[at] for at in EARLY_B]
    a_sp, b_sp = pl.pallas_call(
        early_kernel,
        out_shape=(halves, halves),
        in_specs=[scalars] + [local] * len(early),
        out_specs=(local, local),
        compiler_params=pltpu.CompilerParams(vmem_limit_bytes=24 << 20),
        name="early",
    )(ints, *early)
    count = len(a_blocks) + len(b_blocks)
    return pl.pallas_call(
        kernel,
        out_shape=(jax.ShapeDtypeStruct((RESULTS, SIDE, SIDE), jnp.float32), halves, halves),
        in_specs=[scalars] + [local] * (count + 2),
        out_specs=(local, local, local),
        input_output_aliases={count + 1: 1, count + 2: 2},
        scratch_shapes=[
            pltpu.SMEM((4 * RING, 8, 128), jnp.float32),
            pltpu.SMEM((STEPS * SLOTS * SLOTS,), jnp.float32),
            pltpu.VMEM((4 * RING, 8, 128), jnp.float32),
            pltpu.SemaphoreType.DMA,
        ],
        compiler_params=pltpu.CompilerParams(vmem_limit_bytes=24 << 20),
        name="multiply",
    )(ints, *a_blocks, *b_blocks, a_sp, b_sp)[0]


def program(a_tiles, b_tiles, a_rows, b_cols, c_shape, pairs, pair_count):
    col, row = lax.axis_index("col"), lax.axis_index("row")
    ints = jnp.concatenate(
        [
            c_shape.reshape(-1),
            pairs.reshape(-1),
            pair_count.reshape(-1),
            col.astype(jnp.int32)[None],
            row.astype(jnp.int32)[None],
            jnp.array(HEAD_AT + REST_AT, jnp.int32),
        ]
    )

    a_own = scatter(a_tiles[0, 0], a_rows[0, 0], "col", col)
    b_first = scatter(b_tiles[0, 0], b_cols[0, 0], "row", row)
    b_first, ints = lax.optimization_barrier((b_first, ints))
    b_own = b_first + sum(lax.ppermute(b_first, "row", to_plane(z)) for z in range(1, PLANES))

    block = jnp.concatenate([a_own, lax.ppermute(a_own, "col", SWAP_Z)])
    a_blocks, after, before = [block], block, block
    for _ in range(1, RING // 2):
        after = lax.ppermute(after, ("row", "col"), ring_x(1))
        before = lax.ppermute(before, ("row", "col"), ring_x(-1))
        a_blocks += [after, before]
    a_blocks.append(lax.ppermute(after, ("row", "col"), ring_x(1)))

    behind = lax.ppermute(b_own, "row", ring_y(1))
    ahead = lax.ppermute(b_own, "row", ring_y(-1))
    near = jnp.concatenate([behind, b_own, ahead])
    back = lax.ppermute(near, "row", ring_y(3))
    front = lax.ppermute(near[SHARD:], "row", ring_y(-2))
    mine = [back, near, front]
    other = [lax.ppermute(part, "row", SWAP_CORE) for part in mine]

    return multiply(ints, a_blocks, mine + other)[None, None]


def solution(mesh):
    return jax.shard_map(
        program,
        mesh=mesh,
        in_specs=(
            P("row", "col", None, None, None),
            P("row", "col", None, None, None),
            P("row", "col", None),
            P("row", "col", None),
            P("row", "col", None, None),
            P("row", "col", None, None, None),
            P("row", "col", None),
        ),
        out_specs=P("row", "col", None, None, None),
        check_vma=False,
    )
```
